32 devices in a mesh: dp: 4 (over x, core), expert: 8 (over z, y).
Axes of the slice: x: 2, y: 2, z: 4, core: 2. Of those that a mesh axis runs over, the one named last changes fastest.
Arguments:
- tokens: bfloat16 [4096, 2048], P(('dp', 'expert')), may hold values from -6 to 6
- upstream: bfloat16 [4096, 2048], P(('dp', 'expert')), may hold values from -1.1953125 to 1.1953125
- expert_ids: int32 [4096, 3], P(('dp', 'expert')), may hold values from 0 to 7, all different within a row; in each aligned block of 128 rows (0 to 127, 128 to 255, ...) at most 64 rows name the same one
- gate_probs: float32 [4096, 3], P(('dp', 'expert')), may hold values from 0.05 to 1
- w_gate: bfloat16 [8, 2048, 704], P('expert'), may hold values from -0.125 to 0.125
- w_up: bfloat16 [8, 2048, 704], P('expert'), may hold values from -0.125 to 0.125
- w_down: bfloat16 [8, 704, 2048], P('expert'), may hold values from -0.21875 to 0.21875
Outputs:
- mixed: bfloat16 [4096, 2048], P(('dp', 'expert'))
- grad_probs: float32 [4096, 3], P(('dp', 'expert'))
- token_grad: bfloat16 [4096, 2048], P(('dp', 'expert'))
- grad_gate: float32 [8, 2048, 704], P('expert', 'dp')
- grad_up: float32 [8, 2048, 704], P('expert', 'dp')
- grad_down: float32 [8, 704, 2048], P('expert', None, 'dp')
The draws below stay inside these ranges and needn't reach their ends.
Inputs may be any that keep to these rules, and one draw needn't show every extreme that they name: `expert_ids`: each token names 3 different experts. Within each aligned block of 128 tokens (the tokens of one device) at most 64 routes name one expert, and in some blocks one expert is named by exactly 64 routes.
All inputs are finite; a program needn't handle non-finite values.
Results may differ from the reference program's by a relative error of at most 0.015.
Values may be sent and summed in bfloat16 or wider, within the bound.
A program may use at most 128 MiB of HBM per device.

```python
import math
import jax
import jax.numpy as jnp
import numpy as np
from jax import lax

D = 2048
FFW = 704
TOPW = 3
TOK_DEV = 128
EXPERTS = 8
CAP = 64
TOKENS = 4096
N_DP = 4


def block_levels(rng, extent, shards, low, high):
    def one(position, blocks):
        heights = jax.random.uniform(jax.random.fold_in(jax.random.fold_in(rng, 6), position), (blocks,), jnp.float32, low / len(shards), high / len(shards))
        return jnp.repeat(jnp.exp(heights), extent[position] // blocks).reshape((-1,) + (1,) * (len(extent) - position - 1))

    level = one(*shards[0])
    for cut in shards[1:]:
        level = level * one(*cut)
    return level


def routed_block(own_key, own, number, rows, number_of, top, reach, lean):
    ranking = jax.random.permutation(own_key, number_of)
    crowded, ordinary = shares(number_of, rows * top, reach, lean, True), shares(number_of, rows * top, reach, lean, False)
    places = jnp.arange(number_of)

    def named(sizes, rotation):
        used = int((sizes > 0).sum())
        fixed = max(1, used // 4)
        shifted = fixed + (places - fixed + rotation * (used - fixed)) % max(1, number_of - fixed)
        return jnp.zeros((number_of,), jnp.int32).at[ranking[jnp.where(places < fixed, places, shifted)]].set(jnp.asarray(sizes, jnp.int32))

    sizes = jnp.where(number % 4 == 0, named(crowded, number // 4), named(ordinary, number - number // 4 - 1))
    mixed = jax.random.permutation(jax.random.fold_in(own, 3), number_of)
    source_of, sink = mixed[0:number_of // 2 * 2:2], mixed[1:number_of // 2 * 2:2]
    margin = jnp.minimum(sizes[source_of] - 1, reach - sizes[sink]) // 2
    margin = jnp.where((source_of == ranking[0]) | (sink == ranking[0]) | (sizes[sink] == 0), 0, jnp.maximum(margin, 0))
    shifted = jax.random.randint(jax.random.fold_in(own, 4), (number_of // 2,), 0, 1 << 20) % (margin + 1)
    sizes = sizes.at[source_of].add(-shifted).at[sink].add(shifted)
    labels = jnp.searchsorted(jnp.cumsum(sizes), jnp.arange(rows * top), side="right").astype(jnp.int32)
    listing = labels.reshape(top, rows).T
    listing = listing[jax.random.permutation(jax.random.fold_in(own, 1), rows)]
    rotation = jax.random.randint(jax.random.fold_in(own, 2), (rows, 1), 0, top)
    return jnp.take_along_axis(listing, (jnp.arange(top)[None, :] + rotation) % top, axis=1)


def shares(amount, total, most, skew, full):
    weights = [(1 << 20) // math.isqrt(standing ** skew) + 1 for standing in range(1, amount + 1)]
    largest = most if full else min(most, max(-(-total // amount), total * weights[0] // sum(weights)))
    least = 1 if total - largest >= amount - 1 else 0
    given, surplus = [largest] + [least] * (amount - 1), total - largest - least * (amount - 1)
    while surplus > 0:
        movable = [i for i in range(1, amount) if given[i] < largest] or [i for i in range(1, amount) if given[i] < most]
        whole, budget = sum([weights[i] for i in movable]), surplus
        for i in movable:
            addition = min(most - given[i], max(1, budget * weights[i] // whole), surplus)
            given[i] = given[i] + addition
            surplus = surplus - addition
    return np.array(given)


def scatter_about(stream_key, dims, spread, most, pieces=(), kind=jnp.bfloat16):
    level = block_levels(stream_key, dims, pieces, -0.22, 0.18) if pieces else 1.0
    entries = jax.random.normal(stream_key, dims, jnp.float32) * spread * level
    return jnp.minimum(jnp.maximum(entries, -most), most).astype(kind)


def setup_inputs(seed: int = 0) -> dict:
    keys = jax.random.split(jax.random.key(seed), 8)
    tokens = scatter_about(keys[0], (TOKENS, D), 1.0, 6.0, ((0, 32),))
    upstream = scatter_about(keys[1], (TOKENS, D), 0.2, 1.1953125, ((0, 32),))
    expert_ids_keys = jax.random.split(jax.random.fold_in(keys[2], 1), TOKENS // TOK_DEV)
    expert_ids_turns = jax.random.permutation(jax.random.fold_in(keys[2], 3), TOKENS // TOK_DEV)
    expert_ids = jax.vmap(lambda own, number: routed_block(jax.random.fold_in(keys[2], 2), own, number, TOK_DEV, EXPERTS, TOPW, CAP, 2))(expert_ids_keys, expert_ids_turns).reshape((TOKENS, TOPW))
    gate_probs = jnp.clip(jnp.exp(math.log(1.0) - 2.9957323 * jax.random.uniform(keys[3], (TOKENS, TOPW), jnp.float32) ** block_levels(keys[3], (TOKENS, TOPW), ((0, 32),), -0.2, 0.2)), 0.05, 1.0)
    w_gate = scatter_about(keys[4], (EXPERTS, D, FFW), D ** -0.5, 0.125, ((0, 8),))
    w_up = scatter_about(keys[5], (EXPERTS, D, FFW), D ** -0.5, 0.125, ((0, 8),))
    w_down = scatter_about(keys[6], (EXPERTS, FFW, D), FFW ** -0.5, 0.21875, ((0, 8),))
    return dict(tokens=tokens, upstream=upstream, expert_ids=expert_ids, gate_probs=gate_probs, w_gate=w_gate, w_up=w_up, w_down=w_down)


def slots_of(block_ids):
    matches = (block_ids[:, None] == jnp.arange(EXPERTS, dtype=jnp.int32)[None, :]).astype(jnp.int32)
    before = jnp.cumsum(matches, axis=0) - matches
    return jnp.sum(before * matches, axis=1).astype(jnp.int32)


def expert_forward(row_data, gate_matrix, up_matrix, down_matrix):
    gate_pre = jnp.dot(row_data, gate_matrix, preferred_element_type=jnp.float32)
    up_pre = jnp.dot(row_data, up_matrix, preferred_element_type=jnp.float32)
    hidden = (jax.nn.silu(gate_pre) * up_pre).astype(jnp.bfloat16)
    result = jnp.dot(hidden, down_matrix, preferred_element_type=jnp.float32).astype(jnp.bfloat16)
    return result, gate_pre, up_pre, hidden


def expert_backward(out_grad, gate_pre, up_pre, gate_matrix, up_matrix, down_matrix):
    hidden_grad = jnp.dot(out_grad, down_matrix.T, preferred_element_type=jnp.float32)
    sigmoid_gate = jax.nn.sigmoid(gate_pre)
    gate_grad = (hidden_grad * up_pre * sigmoid_gate * (1.0 + gate_pre * (1.0 - sigmoid_gate))).astype(jnp.bfloat16)
    up_grad = (hidden_grad * gate_pre * sigmoid_gate).astype(jnp.bfloat16)
    route_grad = (jnp.dot(gate_grad, gate_matrix.T, preferred_element_type=jnp.float32)
                  + jnp.dot(up_grad, up_matrix.T, preferred_element_type=jnp.float32)).astype(jnp.bfloat16)
    return route_grad, gate_grad, up_grad


def group_sums(left, right):
    partial_value = jnp.einsum("gmi,gmf->gif", left.astype(jnp.float32), right.astype(jnp.float32),
                         precision=lax.Precision.HIGHEST)
    rounded = lax.optimization_barrier(partial_value.astype(jnp.bfloat16))
    return jnp.sum(rounded.astype(jnp.float32), axis=0)


def reference(tokens, upstream, expert_ids, gate_probs, w_gate, w_up, w_down):
    block_count = TOKENS // TOK_DEV
    routes = TOK_DEV * TOPW
    block_ids = expert_ids.reshape(block_count, routes)
    slot = jax.vmap(slots_of)(block_ids)
    target = block_ids * CAP + slot
    inverse = jnp.full((block_count, EXPERTS * CAP), routes, jnp.int32)
    inverse = inverse.at[jnp.arange(block_count, dtype=jnp.int32)[:, None], target].set(
        jnp.broadcast_to(jnp.arange(routes, dtype=jnp.int32)[None, :], (block_count, routes)))
    flat_probs = gate_probs.reshape(-1)
    block_base = (jnp.arange(block_count, dtype=jnp.int32) * routes)[:, None]

    def per_expert(expert):
        route_index = lax.dynamic_slice_in_dim(inverse, expert * CAP, CAP, 1)
        is_live = route_index < routes
        safe_index = jnp.minimum(route_index, routes - 1) + block_base
        token_index = (safe_index // TOPW).reshape(-1)
        live_flat = is_live.reshape(-1)
        expert_rows = jnp.where(live_flat[:, None], jnp.take(tokens, token_index, axis=0),
                                jnp.zeros((), tokens.dtype))
        upstream_rows = jnp.take(upstream, token_index, axis=0)
        weight_rows = jnp.where(live_flat, jnp.take(flat_probs, safe_index.reshape(-1)), 0.0)
        out_grad = (weight_rows[:, None] * upstream_rows.astype(jnp.float32)).astype(jnp.bfloat16)
        gate_matrix = w_gate[expert]
        up_matrix = w_up[expert]
        down_matrix = w_down[expert]
        result, gate_pre, up_pre, hidden = expert_forward(expert_rows, gate_matrix, up_matrix, down_matrix)
        route_grad, gate_grad, up_grad = expert_backward(out_grad, gate_pre, up_pre, gate_matrix, up_matrix, down_matrix)
        grouped_rows = expert_rows.reshape(N_DP, -1, D)
        gate_sum = group_sums(grouped_rows, gate_grad.reshape(N_DP, -1, FFW))
        up_sum = group_sums(grouped_rows, up_grad.reshape(N_DP, -1, FFW))
        down_sum = group_sums(hidden.reshape(N_DP, -1, FFW), out_grad.reshape(N_DP, -1, D))
        return (result.reshape(block_count, CAP, D), route_grad.reshape(block_count, CAP, D),
                gate_sum, up_sum, down_sum)

    outputs_all, grads_all, grad_gate, grad_up, grad_down = lax.map(per_expert, jnp.arange(EXPERTS, dtype=jnp.int32))
    probs_blocks = gate_probs.reshape(block_count, TOK_DEV, TOPW)
    upstream_blocks = upstream.reshape(block_count, TOK_DEV, D)

    def per_block(block):
        ids_here = block_ids[block]
        slot_here = slot[block]
        routed_out = outputs_all[ids_here, block, slot_here].reshape(TOK_DEV, TOPW, D).astype(jnp.float32)
        routed_grad = grads_all[ids_here, block, slot_here].reshape(TOK_DEV, TOPW, D).astype(jnp.float32)
        mixed_here = jnp.sum(probs_blocks[block][:, :, None] * routed_out, axis=1).astype(jnp.bfloat16)
        probs_grad = jnp.sum(upstream_blocks[block][:, None, :].astype(jnp.float32) * routed_out, axis=2)
        token_here = jnp.sum(routed_grad, axis=1).astype(jnp.bfloat16)
        return mixed_here, probs_grad, token_here

    mixed, grad_probs, token_grad = lax.map(per_block, jnp.arange(block_count, dtype=jnp.int32))
    return (mixed.reshape(TOKENS, D), grad_probs.reshape(TOKENS, TOPW), token_grad.reshape(TOKENS, D),
            grad_gate, grad_up, grad_down)
```

```python
import jax
import jax.numpy as jnp
from jax import lax
from jax.sharding import PartitionSpec as P

F32 = jnp.float32
BF16 = jnp.bfloat16


def dot(left, right, dims):
    return lax.dot_general(left, right, (dims, ((), ())), preferred_element_type=F32)


def shards(tokens, upstream, expert_ids, gate_probs, w_gate, w_up, w_down):
    tok_rows, width = tokens.shape
    routes = expert_ids.shape[1]
    experts = lax.axis_size("expert")
    capacity = 4 * tok_rows * routes // (3 * experts)
    w_gate, w_up, w_down = w_gate[0], w_up[0], w_down[0]

    picks = expert_ids[None] == jnp.arange(experts, dtype=jnp.int32)[:, None, None]
    dense = jnp.sum(jnp.where(picks, gate_probs[None], 0.0), axis=2)
    dense = jnp.where(jnp.any(picks, axis=2), dense, -1.0)
    probs = lax.all_to_all(dense, "expert", split_axis=0, concat_axis=0, tiled=True)

    all_tokens = lax.all_gather(tokens, "expert")
    all_upstream = lax.all_gather(upstream, "expert")

    routed = probs >= 0.0
    counts = routed.astype(jnp.int32)
    slot = jnp.cumsum(counts, axis=1) - counts
    chosen = routed[:, None, :] & (
        slot[:, None, :] == jnp.arange(capacity, dtype=jnp.int32)[None, :, None]
    )
    select = chosen.astype(BF16)
    row_probs = jnp.sum(jnp.where(chosen, probs[:, None, :], 0.0), axis=2).reshape(-1, 1)

    def pick(values):
        return (
            jnp.einsum("bct,btd->bcd", select, values, preferred_element_type=F32)
            .astype(BF16)
            .reshape(experts * capacity, width)
        )

    def spread(rows):
        rows = rows.reshape(experts, capacity, width)
        return jnp.einsum("bct,bcd->btd", select, rows, preferred_element_type=F32).astype(BF16)

    rows = pick(all_tokens)
    gate_pre = dot(rows, w_gate, ((1,), (0,)))
    up_pre = dot(rows, w_up, ((1,), (0,)))
    sig = jax.nn.sigmoid(gate_pre)
    hidden = (gate_pre * sig * up_pre).astype(BF16)
    weighted = (dot(hidden, w_down, ((1,), (0,))) * row_probs).astype(BF16)
    mixed = lax.psum_scatter(spread(weighted), "expert", scatter_dimension=0)

    grads = pick(all_upstream)
    raw = dot(grads, w_down, ((1,), (1,)))
    row_dots = jnp.sum(raw * hidden.astype(F32), axis=1).reshape(experts, capacity, 1)
    hidden_grad = raw * row_probs
    gate_grad = (hidden_grad * up_pre * sig * (1.0 + gate_pre * (1.0 - sig))).astype(BF16)
    up_grad = (hidden_grad * gate_pre * sig).astype(BF16)
    scaled_hidden = (hidden.astype(F32) * row_probs).astype(BF16)
    route_grad = (
        dot(gate_grad, w_gate, ((1,), (1,))) + dot(up_grad, w_up, ((1,), (1,)))
    ).astype(BF16)
    token_grad = lax.psum_scatter(spread(route_grad), "expert", scatter_dimension=0)

    token_dots = jnp.sum(jnp.where(chosen, row_dots, 0.0), axis=1)
    back = lax.all_to_all(token_dots, "expert", split_axis=0, concat_axis=0, tiled=True)
    grad_probs = jnp.sum(jnp.where(picks, back[:, :, None], 0.0), axis=0)

    def scatter(partial, dim):
        return lax.psum_scatter(
            partial[None].astype(BF16), "dp", scatter_dimension=dim, tiled=True
        ).astype(F32)

    grad_gate = scatter(dot(rows, gate_grad, ((0,), (0,))), 1)
    grad_up = scatter(dot(rows, up_grad, ((0,), (0,))), 1)
    grad_down = scatter(dot(scaled_hidden, grads, ((0,), (0,))), 2)
    return (mixed, grad_probs, token_grad, grad_gate, grad_up, grad_down)


def solution(mesh):
    rows = P(("dp", "expert"), None)
    weights = P("expert", None, None)
    return jax.shard_map(
        shards,
        mesh=mesh,
        in_specs=(rows, rows, rows, rows, weights, weights, weights),
        out_specs=(
            rows,
            rows,
            rows,
            P("expert", "dp", None),
            P("expert", "dp", None),
            P("expert", None, "dp"),
        ),
        check_vma=False,
    )
```

```python
import jax
import jax.numpy as jnp
from jax import lax
from jax.sharding import PartitionSpec as P

F32 = jnp.float32
BF16 = jnp.bfloat16


def dot(left, right, dims):
    return lax.dot_general(left, right, (dims, ((), ())), preferred_element_type=F32)


def shards(tokens, upstream, expert_ids, gate_probs, w_gate, w_up, w_down):
    tok_rows, width = tokens.shape
    routes = expert_ids.shape[1]
    experts = lax.axis_size("expert")
    capacity = 4 * tok_rows * routes // (3 * experts)
    w_gate, w_up, w_down = w_gate[0], w_up[0], w_down[0]

    ids = jnp.transpose(expert_ids)
    picks = ids[None] == jnp.arange(experts, dtype=jnp.int32)[:, None, None]
    routed = jnp.any(picks, axis=1)
    dense = jnp.sum(jnp.where(picks, jnp.transpose(gate_probs)[None], 0.0), axis=1)
    counts = routed.astype(F32)
    earlier = jnp.arange(tok_rows)[:, None] < jnp.arange(tok_rows)[None, :]
    slot = dot(counts.astype(BF16), earlier.astype(BF16), ((1,), (0,))).astype(jnp.int32)
    chosen = routed[:, None, :] & (
        slot[:, None, :] == jnp.arange(capacity, dtype=jnp.int32)[None, :, None]
    )
    select = chosen.astype(BF16).reshape(experts * capacity, tok_rows)
    send_probs = jnp.sum(jnp.where(chosen, dense[:, None, :], 0.0), axis=2)

    def exchange(values):
        return lax.all_to_all(
            values.reshape(experts, capacity, -1), "expert", split_axis=0, concat_axis=0, tiled=True
        ).reshape(experts * capacity, -1)

    rows = exchange(dot(select, tokens, ((1,), (0,))).astype(BF16))
    out_grad = dot(select, upstream, ((1,), (0,))) * send_probs.reshape(-1, 1)
    grads = exchange(out_grad.astype(BF16))

    gate_pre = dot(rows, w_gate, ((1,), (0,)))
    up_pre = dot(rows, w_up, ((1,), (0,)))
    sig = jax.nn.sigmoid(gate_pre)
    hidden = (gate_pre * sig * up_pre).astype(BF16)
    result = dot(hidden, w_down, ((1,), (0,))).astype(BF16)
    back_out = exchange(result)

    hidden_grad = dot(grads, w_down, ((1,), (1,)))
    gate_grad = (hidden_grad * up_pre * sig * (1.0 + gate_pre * (1.0 - sig))).astype(BF16)
    up_grad = (hidden_grad * gate_pre * sig).astype(BF16)

    def scatter(partial, dim):
        partial = partial[None].astype(BF16)
        return lax.psum_scatter(partial, "dp", scatter_dimension=dim, tiled=True).astype(F32)

    grad_gate = scatter(dot(rows, gate_grad, ((0,), (0,))), 1)
    grad_up = scatter(dot(rows, up_grad, ((0,), (0,))), 1)
    grad_down = scatter(dot(hidden, grads, ((0,), (0,))), 2)
    route_grad = (
        dot(gate_grad, w_gate, ((1,), (1,))) + dot(up_grad, w_up, ((1,), (1,)))
    ).astype(BF16)
    back_grad = exchange(route_grad)

    sent_up = dot(select, upstream, ((1,), (0,)))
    mixed_rows = (back_out.astype(F32) * send_probs.reshape(-1, 1)).astype(BF16)
    mixed = dot(select, mixed_rows, ((0,), (0,))).astype(BF16)
    row_dots = jnp.sum(sent_up * back_out.astype(F32), axis=1).reshape(experts, capacity, 1)
    token_dots = jnp.sum(jnp.where(chosen, row_dots, 0.0), axis=1)
    grad_probs = jnp.transpose(jnp.sum(jnp.where(picks, token_dots[:, None, :], 0.0), axis=0))
    token_grad = dot(select, back_grad, ((0,), (0,))).astype(BF16)
    return (mixed, grad_probs, token_grad, grad_gate, grad_up, grad_down)


def solution(mesh):
    rows = P(("dp", "expert"), None)
    weights = P("expert", None, None)
    return jax.shard_map(
        shards,
        mesh=mesh,
        in_specs=(rows, rows, rows, rows, weights, weights, weights),
        out_specs=(
            rows,
            rows,
            rows,
            P("expert", "dp", None),
            P("expert", "dp", None),
            P("expert", None, "dp"),
        ),
        check_vma=False,
    )
```

```python
import jax
import jax.numpy as jnp
from jax import lax
from jax.sharding import PartitionSpec as P

F32 = jnp.float32
BF16 = jnp.bfloat16


def dot(left, right, dims):
    return lax.dot_general(left, right, (dims, ((), ())), preferred_element_type=F32)


def shards(tokens, upstream, expert_ids, gate_probs, w_gate, w_up, w_down):
    tok_rows, width = tokens.shape
    routes = expert_ids.shape[1]
    experts = lax.axis_size("expert")
    capacity = 4 * tok_rows * routes // (3 * experts)
    w_gate, w_up, w_down = w_gate[0], w_up[0], w_down[0]

    ids = jnp.transpose(expert_ids)
    picks = ids[None] == jnp.arange(experts, dtype=jnp.int32)[:, None, None]
    routed = jnp.any(picks, axis=1)
    dense = jnp.sum(jnp.where(picks, jnp.transpose(gate_probs)[None], 0.0), axis=1)
    counts = routed.astype(F32)
    earlier = jnp.arange(tok_rows)[:, None] < jnp.arange(tok_rows)[None, :]
    slot = dot(counts.astype(BF16), earlier.astype(BF16), ((1,), (0,))).astype(jnp.int32)
    chosen = routed[:, None, :] & (
        slot[:, None, :] == jnp.arange(capacity, dtype=jnp.int32)[None, :, None]
    )
    select = chosen.astype(BF16).reshape(experts * capacity, tok_rows)
    send_probs = jnp.sum(jnp.where(chosen, dense[:, None, :], 0.0), axis=2)

    def exchange(values):
        return lax.all_to_all(
            values.reshape(experts, capacity, -1), "expert", split_axis=0, concat_axis=0, tiled=True
        ).reshape(experts * capacity, -1)

    rows = exchange(dot(select, tokens, ((1,), (0,))).astype(BF16))
    out_grad = dot(select, upstream, ((1,), (0,))) * send_probs.reshape(-1, 1)
    grads = exchange(out_grad.astype(BF16))

    gate_pre = dot(rows, w_gate, ((1,), (0,)))
    up_pre = dot(rows, w_up, ((1,), (0,)))
    sig = jax.nn.sigmoid(gate_pre)
    hidden = (gate_pre * sig * up_pre).astype(BF16)
    result = dot(hidden, w_down, ((1,), (0,))).astype(BF16)

    hidden_grad = dot(grads, w_down, ((1,), (1,)))
    gate_grad = (hidden_grad * up_pre * sig * (1.0 + gate_pre * (1.0 - sig))).astype(BF16)
    up_grad = (hidden_grad * gate_pre * sig).astype(BF16)

    def scatter(partial, dim):
        partial = partial.astype(BF16)
        far = lax.axis_size("dp") // 2
        shape = partial.shape[:dim] + (far, 2, partial.shape[dim] // far // 2) + partial.shape[dim + 1 :]
        pairs = [[2 * i, 2 * i + 1] for i in range(far)]
        half = lax.psum_scatter(
            partial.reshape(shape), "dp", scatter_dimension=dim + 1, axis_index_groups=pairs
        )
        chips = [[2 * i + c for i in range(far)] for c in range(2)]
        return lax.psum_scatter(
            half, "dp", scatter_dimension=dim, axis_index_groups=chips
        ).astype(F32)[None]

    part_gate = dot(rows, gate_grad, ((0,), (0,))).astype(BF16)
    part_up = dot(rows, up_grad, ((0,), (0,))).astype(BF16)
    part_down = dot(hidden, grads, ((0,), (0,))).astype(BF16)
    result, part_gate, part_up, part_down = lax.optimization_barrier(
        (result, part_gate, part_up, part_down)
    )
    grad_gate = scatter(part_gate, 0)
    grad_up = scatter(part_up, 0)
    grad_down = scatter(part_down, 1)
    back_out = exchange(result)
    route_grad = (
        dot(gate_grad, w_gate, ((1,), (1,))) + dot(up_grad, w_up, ((1,), (1,)))
    ).astype(BF16)
    back_grad = exchange(route_grad)

    sent_up = dot(select, upstream, ((1,), (0,)))
    mixed_rows = (back_out.astype(F32) * send_probs.reshape(-1, 1)).astype(BF16)
    mixed = dot(select, mixed_rows, ((0,), (0,))).astype(BF16)
    row_dots = jnp.sum(sent_up * back_out.astype(F32), axis=1).reshape(experts, capacity, 1)
    token_dots = jnp.sum(jnp.where(chosen, row_dots, 0.0), axis=1)
    grad_probs = jnp.transpose(jnp.sum(jnp.where(picks, token_dots[:, None, :], 0.0), axis=0))
    token_grad = dot(select, back_grad, ((0,), (0,))).astype(BF16)
    return (mixed, grad_probs, token_grad, grad_gate, grad_up, grad_down)


def solution(mesh):
    rows = P(("dp", "expert"), None)
    weights = P("expert", None, None)
    return jax.shard_map(
        shards,
        mesh=mesh,
        in_specs=(rows, rows, rows, rows, weights, weights, weights),
        out_specs=(
            rows,
            rows,
            rows,
            P("expert", "dp", None),
            P("expert", "dp", None),
            P("expert", None, "dp"),
        ),
        check_vma=False,
    )
```

```python
import functools

import jax
import jax.numpy as jnp
from jax import lax
from jax.experimental import pallas as pl
from jax.experimental.pallas import tpu as pltpu
from jax.sharding import PartitionSpec as P

F32 = jnp.float32
BF16 = jnp.bfloat16


def dot(left, right, dims):
    return lax.dot_general(left, right, (dims, ((), ())), preferred_element_type=F32)


def columns(experts):
    near = 1 << ((experts.bit_length() - 1) // 2)
    return experts // near, near


def gather_kernel(
    nz, ny, capacity, tok_ref, ups_ref, plan_ref, out_ref,
    held, plans, staged, send_sem, recv_sem, psend_sem, precv_sem, ysend_sem, yrecv_sem,
):
    me = lax.axis_index("expert")
    z, y = me // ny, lax.rem(me, ny)
    steps = 2 * nz

    def step_of(z_to, y_to):
        return {"expert": z_to * ny + y_to}

    def hop(i, s, k, way):
        z_to = lax.rem(z + (1 if way == 0 else nz - 1), nz)
        return pltpu.make_async_remote_copy(
            held.at[i, s], held.at[i, s], send_sem.at[i, k, way], recv_sem.at[i, s],
            device_id=step_of(z_to, y), device_id_type=pl.DeviceIdType.MESH,
        )

    def plan_hop(s, k, way):
        z_to = lax.rem(z + (1 if way == 0 else nz - 1), nz)
        return pltpu.make_async_remote_copy(
            plans.at[s], plans.at[s], psend_sem.at[k, way], precv_sem.at[s],
            device_id=step_of(z_to, y), device_id_type=pl.DeviceIdType.MESH,
        )

    def across(i, s, dy):
        return pltpu.make_async_remote_copy(
            staged.at[i, s, dy - 1], out_ref.at[i, s * ny + y],
            ysend_sem.at[i, s, dy - 1], yrecv_sem.at[i, s, dy - 1],
            device_id=step_of(z, lax.rem(y + dy, ny)), device_id_type=pl.DeviceIdType.MESH,
        )

    barrier = pltpu.get_barrier_semaphore()

    def greet(z_to, y_to):
        pl.semaphore_signal(
            barrier, inc=1, device_id=step_of(z_to, y_to), device_id_type=pl.DeviceIdType.MESH
        )

    for dy in range(1, ny):
        greet(z, lax.rem(y + dy, ny))

    greet(lax.rem(z + 1, nz), y)
    greet(lax.rem(z + nz - 1, nz), y)

    held[0, z] = tok_ref[...]
    held[1, z] = ups_ref[...]
    plans[z] = plan_ref[...]

    pl.semaphore_wait(barrier, ny + 1)

    def process(i, s):
        line = lax.broadcasted_iota(jnp.int32, (capacity, tok_ref.shape[0]), 0).astype(F32)
        for dy in list(range(1, ny)) + [0]:
            plan = plans[s, z * ny + lax.rem(y + dy, ny)]
            hit = line == plan[0:1, :]
            weight = jnp.where(i == 0, jnp.ones_like(plan[1:2, :]), plan[1:2, :])
            scale = jnp.sum(jnp.where(hit, weight, 0.0), axis=1, keepdims=True)
            got = jnp.dot(
                jnp.where(hit, 1.0, 0.0).astype(BF16), held[i, s], preferred_element_type=F32
            )
            value = (got * scale).astype(BF16)
            if dy == 0:
                out_ref[i, s * ny + y] = value
            else:
                staged[i, s, dy - 1] = value
                across(i, s, dy).start()

    def body(q, carry):
        i, k = q // nz, lax.rem(q, nz)
        low, high = z - k, z + k

        @pl.when(low >= 0)
        def _():
            @pl.when(k > 0)
            def _():
                @pl.when(i == 0)
                def _():
                    plan_hop(low, k, 0).wait_recv()

                hop(i, low, k, 0).wait_recv()

            @pl.when(z < nz - 1)
            def _():
                @pl.when(i == 0)
                def _():
                    plan_hop(low, k, 0).start()

                hop(i, low, k, 0).start()

        @pl.when(high < nz)
        def _():
            @pl.when(k > 0)
            def _():
                @pl.when(i == 0)
                def _():
                    plan_hop(high, k, 1).wait_recv()

                hop(i, high, k, 1).wait_recv()

            @pl.when(z > 0)
            def _():
                @pl.when(i == 0)
                def _():
                    plan_hop(high, k, 1).start()

                hop(i, high, k, 1).start()

        @pl.when(low >= 0)
        def _():
            process(i, low)

        @pl.when((high < nz) & (k > 0))
        def _():
            process(i, high)

        return carry

    lax.fori_loop(0, steps, body, 0)

    def finish(q, carry):
        i, k = q // nz, lax.rem(q, nz)
        low, high = z - k, z + k

        @pl.when((low >= 0) & (z < nz - 1))
        def _():
            @pl.when(i == 0)
            def _():
                plan_hop(low, k, 0).wait_send()

            hop(i, low, k, 0).wait_send()

        @pl.when((high < nz) & (z > 0))
        def _():
            @pl.when(i == 0)
            def _():
                plan_hop(high, k, 1).wait_send()

            hop(i, high, k, 1).wait_send()

        for dy in range(1, ny):
            across(i, k, dy).wait_send()
            across(i, k, dy).wait_recv()
        return carry

    lax.fori_loop(0, steps, finish, 0)


def gather(tokens, upstream, plan, capacity):
    tok_rows, width = tokens.shape
    experts = plan.shape[0]
    nz, ny = columns(experts)
    peers = max(ny - 1, 1)
    vmem = pl.BlockSpec(memory_space=pltpu.VMEM)
    dma = pltpu.SemaphoreType.DMA
    return pl.pallas_call(
        functools.partial(gather_kernel, nz, ny, capacity),
        out_shape=jax.ShapeDtypeStruct((2, experts, capacity, width), BF16),
        in_specs=[vmem] * 3,
        out_specs=vmem,
        scratch_shapes=[
            pltpu.VMEM((2, nz, tok_rows, width), BF16),
            pltpu.VMEM((nz, experts, 8, tok_rows), F32),
            pltpu.VMEM((2, nz, peers, capacity, width), BF16),
            dma((2, nz, 2)),
            dma((2, nz)),
            dma((nz, 2)),
            dma((nz,)),
            dma((2, nz, peers)),
            dma((2, nz, peers)),
        ],
        compiler_params=pltpu.CompilerParams(
            collective_id=0, has_side_effects=True, vmem_limit_bytes=48 << 20
        ),
        cost_estimate=pl.CostEstimate(
            flops=2 * 2 * experts * capacity * tok_rows * width,
            bytes_accessed=2 * experts * capacity * width * 2 * 4,
            transcendentals=0,
        ),
    )(tokens, upstream, plan)


def shards(tokens, upstream, expert_ids, gate_probs, w_gate, w_up, w_down):
    tok_rows, width = tokens.shape
    routes = expert_ids.shape[1]
    experts = lax.axis_size("expert")
    capacity = 4 * tok_rows * routes // (3 * experts)
    w_gate, w_up, w_down = w_gate[0], w_up[0], w_down[0]

    ids = jnp.transpose(expert_ids)
    picks = ids[None] == jnp.arange(experts, dtype=jnp.int32)[:, None, None]
    routed = jnp.any(picks, axis=1)
    dense = jnp.sum(jnp.where(picks, jnp.transpose(gate_probs)[None], 0.0), axis=1)
    counts = routed.astype(F32)
    earlier = jnp.arange(tok_rows)[:, None] < jnp.arange(tok_rows)[None, :]
    slot = dot(counts.astype(BF16), earlier.astype(BF16), ((1,), (0,))).astype(jnp.int32)
    chosen = routed[:, None, :] & (
        slot[:, None, :] == jnp.arange(capacity, dtype=jnp.int32)[None, :, None]
    )
    select = chosen.astype(BF16).reshape(experts * capacity, tok_rows)
    send_probs = jnp.sum(jnp.where(chosen, dense[:, None, :], 0.0), axis=2)

    def exchange(values):
        return lax.all_to_all(
            values.reshape(experts, capacity, -1), "expert", split_axis=0, concat_axis=0, tiled=True
        ).reshape(experts * capacity, -1)

    code = jnp.where(routed, slot, -1).astype(F32)
    plan = jnp.stack([code, dense] + [jnp.zeros_like(dense)] * 6, axis=1)
    sent = gather(tokens, upstream, plan, capacity)
    rows = sent[0].reshape(experts * capacity, width)
    grads = sent[1].reshape(experts * capacity, width)

    gate_pre = dot(rows, w_gate, ((1,), (0,)))
    up_pre = dot(rows, w_up, ((1,), (0,)))
    sig = jax.nn.sigmoid(gate_pre)
    hidden = (gate_pre * sig * up_pre).astype(BF16)
    result = dot(hidden, w_down, ((1,), (0,))).astype(BF16)

    hidden_grad = dot(grads, w_down, ((1,), (1,)))
    gate_grad = (hidden_grad * up_pre * sig * (1.0 + gate_pre * (1.0 - sig))).astype(BF16)
    up_grad = (hidden_grad * gate_pre * sig).astype(BF16)

    def scatter(partial, dim):
        partial = partial[None]
        return lax.psum_scatter(partial, "dp", scatter_dimension=dim, tiled=True).astype(F32)

    part_gate = dot(rows, gate_grad, ((0,), (0,))).astype(BF16)
    part_up = dot(rows, up_grad, ((0,), (0,))).astype(BF16)
    part_down = dot(hidden, grads, ((0,), (0,))).astype(BF16)
    result, part_gate, part_up, part_down = lax.optimization_barrier(
        (result, part_gate, part_up, part_down)
    )
    grad_gate = scatter(part_gate, 1)
    grad_up = scatter(part_up, 1)
    grad_down = scatter(part_down, 2)
    back_out = exchange(result)
    route_grad = (
        dot(gate_grad, w_gate, ((1,), (1,))) + dot(up_grad, w_up, ((1,), (1,)))
    ).astype(BF16)
    back_grad = exchange(route_grad)

    sent_up = dot(select, upstream, ((1,), (0,)))
    mixed_rows = (back_out.astype(F32) * send_probs.reshape(-1, 1)).astype(BF16)
    mixed = dot(select, mixed_rows, ((0,), (0,))).astype(BF16)
    row_dots = jnp.sum(sent_up * back_out.astype(F32), axis=1).reshape(experts, capacity, 1)
    token_dots = jnp.sum(jnp.where(chosen, row_dots, 0.0), axis=1)
    grad_probs = jnp.transpose(jnp.sum(jnp.where(picks, token_dots[:, None, :], 0.0), axis=0))
    token_grad = dot(select, back_grad, ((0,), (0,))).astype(BF16)
    return (mixed, grad_probs, token_grad, grad_gate, grad_up, grad_down)


def solution(mesh):
    rows = P(("dp", "expert"), None)
    weights = P("expert", None, None)
    return jax.shard_map(
        shards,
        mesh=mesh,
        in_specs=(rows, rows, rows, rows, weights, weights, weights),
        out_specs=(
            rows,
            rows,
            rows,
            P("expert", "dp", None),
            P("expert", "dp", None),
            P("expert", None, "dp"),
        ),
        check_vma=False,
    )
```

```python
import functools

import jax
import jax.numpy as jnp
from jax import lax
from jax.experimental import pallas as pl
from jax.experimental.pallas import tpu as pltpu
from jax.sharding import PartitionSpec as P

F32 = jnp.float32
BF16 = jnp.bfloat16


def dot(left, right, dims):
    return lax.dot_general(left, right, (dims, ((), ())), preferred_element_type=F32)


def columns(experts):
    near = 1 << ((experts.bit_length() - 1) // 2)
    return experts // near, near


def gather_kernel(
    nz, ny, capacity, tok_ref, ups_ref, plan_ref, out_ref,
    held, plans, staged, send_sem, recv_sem, psend_sem, precv_sem, ysend_sem, yrecv_sem,
):
    me = lax.axis_index("expert")
    z, y = me // ny, lax.rem(me, ny)
    steps = 2 * nz

    def step_of(z_to, y_to):
        return {"expert": z_to * ny + y_to}

    def hop(i, s, k, way):
        z_to = lax.rem(z + (1 if way == 0 else nz - 1), nz)
        return pltpu.make_async_remote_copy(
            held.at[i, s], held.at[i, s], send_sem.at[i, k, way], recv_sem.at[i, s],
            device_id=step_of(z_to, y), device_id_type=pl.DeviceIdType.MESH,
        )

    def plan_hop(s, k, way):
        z_to = lax.rem(z + (1 if way == 0 else nz - 1), nz)
        return pltpu.make_async_remote_copy(
            plans.at[s], plans.at[s], psend_sem.at[k, way], precv_sem.at[s],
            device_id=step_of(z_to, y), device_id_type=pl.DeviceIdType.MESH,
        )

    def across(i, s, dy):
        return pltpu.make_async_remote_copy(
            staged.at[i, s, dy - 1], out_ref.at[i, s * ny + y],
            ysend_sem.at[i, s, dy - 1], yrecv_sem.at[i, s, dy - 1],
            device_id=step_of(z, lax.rem(y + dy, ny)), device_id_type=pl.DeviceIdType.MESH,
        )

    barrier = pltpu.get_barrier_semaphore()

    def greet(z_to, y_to):
        pl.semaphore_signal(
            barrier, inc=1, device_id=step_of(z_to, y_to), device_id_type=pl.DeviceIdType.MESH
        )

    for dy in range(1, ny):
        greet(z, lax.rem(y + dy, ny))

    greet(lax.rem(z + 1, nz), y)
    greet(lax.rem(z + nz - 1, nz), y)

    held[0, z] = tok_ref[...]
    held[1, z] = ups_ref[...]
    plans[z] = plan_ref[...]

    pl.semaphore_wait(barrier, ny + 1)

    def process(i, s):
        line = lax.broadcasted_iota(jnp.int32, (capacity, tok_ref.shape[0]), 0).astype(F32)
        for dy in list(range(1, ny)) + [0]:
            plan = plans[s, z * ny + lax.rem(y + dy, ny)]
            hit = line == plan[0:1, :]
            weight = jnp.where(i == 0, jnp.ones_like(plan[1:2, :]), plan[1:2, :])
            scale = jnp.sum(jnp.where(hit, weight, 0.0), axis=1, keepdims=True)
            got = jnp.dot(
                jnp.where(hit, 1.0, 0.0).astype(BF16), held[i, s], preferred_element_type=F32
            )
            value = (got * scale).astype(BF16)
            if dy == 0:
                out_ref[i, s * ny + y] = value
            else:
                staged[i, s, dy - 1] = value
                across(i, s, dy).start()

    def body(q, carry):
        i, k = lax.rem(q, 2), q // 2
        low, high = z - k, z + k

        @pl.when(low >= 0)
        def _():
            @pl.when(k > 0)
            def _():
                @pl.when(i == 0)
                def _():
                    plan_hop(low, k, 0).wait_recv()

                hop(i, low, k, 0).wait_recv()

            @pl.when(z < nz - 1)
            def _():
                @pl.when(i == 0)
                def _():
                    plan_hop(low, k, 0).start()

                hop(i, low, k, 0).start()

        @pl.when(high < nz)
        def _():
            @pl.when(k > 0)
            def _():
                @pl.when(i == 0)
                def _():
                    plan_hop(high, k, 1).wait_recv()

                hop(i, high, k, 1).wait_recv()

            @pl.when(z > 0)
            def _():
                @pl.when(i == 0)
                def _():
                    plan_hop(high, k, 1).start()

                hop(i, high, k, 1).start()

        @pl.when(low >= 0)
        def _():
            process(i, low)

        @pl.when((high < nz) & (k > 0))
        def _():
            process(i, high)

        return carry

    lax.fori_loop(0, steps, body, 0)

    def finish(q, carry):
        i, k = q // nz, lax.rem(q, nz)
        low, high = z - k, z + k

        @pl.when((low >= 0) & (z < nz - 1))
        def _():
            @pl.when(i == 0)
            def _():
                plan_hop(low, k, 0).wait_send()

            hop(i, low, k, 0).wait_send()

        @pl.when((high < nz) & (z > 0))
        def _():
            @pl.when(i == 0)
            def _():
                plan_hop(high, k, 1).wait_send()

            hop(i, high, k, 1).wait_send()

        for dy in range(1, ny):
            across(i, k, dy).wait_send()
            across(i, k, dy).wait_recv()
        return carry

    lax.fori_loop(0, steps, finish, 0)


def gather(tokens, upstream, plan, capacity):
    tok_rows, width = tokens.shape
    experts = plan.shape[0]
    nz, ny = columns(experts)
    peers = max(ny - 1, 1)
    vmem = pl.BlockSpec(memory_space=pltpu.VMEM)
    dma = pltpu.SemaphoreType.DMA
    return pl.pallas_call(
        functools.partial(gather_kernel, nz, ny, capacity),
        out_shape=jax.ShapeDtypeStruct((2, experts, capacity, width), BF16),
        in_specs=[vmem] * 3,
        out_specs=vmem,
        scratch_shapes=[
            pltpu.VMEM((2, nz, tok_rows, width), BF16),
            pltpu.VMEM((nz, experts, 8, tok_rows), F32),
            pltpu.VMEM((2, nz, peers, capacity, width), BF16),
            dma((2, nz, 2)),
            dma((2, nz)),
            dma((nz, 2)),
            dma((nz,)),
            dma((2, nz, peers)),
            dma((2, nz, peers)),
        ],
        compiler_params=pltpu.CompilerParams(
            collective_id=0, has_side_effects=True, vmem_limit_bytes=48 << 20
        ),
        cost_estimate=pl.CostEstimate(
            flops=2 * 2 * experts * capacity * tok_rows * width,
            bytes_accessed=2 * experts * capacity * width * 2 * 4,
            transcendentals=0,
        ),
    )(tokens, upstream, plan)


def shards(tokens, upstream, expert_ids, gate_probs, w_gate, w_up, w_down):
    tok_rows, width = tokens.shape
    routes = expert_ids.shape[1]
    experts = lax.axis_size("expert")
    capacity = 4 * tok_rows * routes // (3 * experts)
    w_gate, w_up, w_down = w_gate[0], w_up[0], w_down[0]

    ids = jnp.transpose(expert_ids)
    picks = ids[None] == jnp.arange(experts, dtype=jnp.int32)[:, None, None]
    routed = jnp.any(picks, axis=1)
    dense = jnp.sum(jnp.where(picks, jnp.transpose(gate_probs)[None], 0.0), axis=1)
    counts = routed.astype(F32)
    earlier = jnp.arange(tok_rows)[:, None] < jnp.arange(tok_rows)[None, :]
    slot = dot(counts.astype(BF16), earlier.astype(BF16), ((1,), (0,))).astype(jnp.int32)
    chosen = routed[:, None, :] & (
        slot[:, None, :] == jnp.arange(capacity, dtype=jnp.int32)[None, :, None]
    )
    select = chosen.astype(BF16).reshape(experts * capacity, tok_rows)
    send_probs = jnp.sum(jnp.where(chosen, dense[:, None, :], 0.0), axis=2)

    def exchange(values):
        return lax.all_to_all(
            values.reshape(experts, capacity, -1), "expert", split_axis=0, concat_axis=0, tiled=True
        ).reshape(experts * capacity, -1)

    code = jnp.where(routed, slot, -1).astype(F32)
    plan = jnp.stack([code, dense] + [jnp.zeros_like(dense)] * 6, axis=1)
    sent = gather(tokens, upstream, plan, capacity)
    rows = sent[0].reshape(experts * capacity, width)
    grads = sent[1].reshape(experts * capacity, width)

    gate_pre = dot(rows, w_gate, ((1,), (0,)))
    up_pre = dot(rows, w_up, ((1,), (0,)))
    sig = jax.nn.sigmoid(gate_pre)
    hidden = (gate_pre * sig * up_pre).astype(BF16)
    result = dot(hidden, w_down, ((1,), (0,))).astype(BF16)

    hidden_grad = dot(grads, w_down, ((1,), (1,)))
    gate_grad = (hidden_grad * up_pre * sig * (1.0 + gate_pre * (1.0 - sig))).astype(BF16)
    up_grad = (hidden_grad * gate_pre * sig).astype(BF16)

    def scatter(partial, dim):
        partial = partial[None]
        return lax.psum_scatter(partial, "dp", scatter_dimension=dim, tiled=True).astype(F32)

    part_gate = dot(rows, gate_grad, ((0,), (0,))).astype(BF16)
    part_up = dot(rows, up_grad, ((0,), (0,))).astype(BF16)
    part_down = dot(hidden, grads, ((0,), (0,))).astype(BF16)
    result, _ = lax.optimization_barrier((result, part_gate))
    grad_gate = scatter(part_gate, 1)
    grad_up = scatter(part_up, 1)
    grad_down = scatter(part_down, 2)
    back_out = exchange(result)
    route_grad = (
        dot(gate_grad, w_gate, ((1,), (1,))) + dot(up_grad, w_up, ((1,), (1,)))
    ).astype(BF16)
    back_grad = exchange(route_grad)

    sent_up = dot(select, upstream, ((1,), (0,)))
    mixed_rows = (back_out.astype(F32) * send_probs.reshape(-1, 1)).astype(BF16)
    mixed = dot(select, mixed_rows, ((0,), (0,))).astype(BF16)
    row_dots = jnp.sum(sent_up * back_out.astype(F32), axis=1).reshape(experts, capacity, 1)
    token_dots = jnp.sum(jnp.where(chosen, row_dots, 0.0), axis=1)
    grad_probs = jnp.transpose(jnp.sum(jnp.where(picks, token_dots[:, None, :], 0.0), axis=0))
    token_grad = dot(select, back_grad, ((0,), (0,))).astype(BF16)
    return (mixed, grad_probs, token_grad, grad_gate, grad_up, grad_down)


def solution(mesh):
    rows = P(("dp", "expert"), None)
    weights = P("expert", None, None)
    return jax.shard_map(
        shards,
        mesh=mesh,
        in_specs=(rows, rows, rows, rows, weights, weights, weights),
        out_specs=(
            rows,
            rows,
            rows,
            P("expert", "dp", None),
            P("expert", "dp", None),
            P("expert", None, "dp"),
        ),
        check_vma=False,
    )
```
